32 devices in a mesh: pipe: 2 (over core), expert: 16 (over z, y, x).
Axes of the slice: x: 2, y: 2, z: 4, core: 2. Of those that a mesh axis runs over, the one named last changes fastest.
Arguments:
- hidden_a: bfloat16 [2, 1024, 3584], P('pipe', 'expert'), may hold values from -6 to 6
- routes_a: int32 [2, 1024, 8], P('pipe', 'expert'), may hold values from 0 to 15, all different within a row; in each aligned block of 64 rows (0 to 63, 64 to 127, ..., all dimensions but the last counted through in order) at most 48 rows name the same one
- hidden_b: bfloat16 [2, 1024, 3584], P('pipe', 'expert'), may hold values from -6 to 6
- routes_b: int32 [2, 1024, 8], P('pipe', 'expert'), may hold values from 0 to 15, all different within a row; in each aligned block of 64 rows (0 to 63, 64 to 127, ..., all dimensions but the last counted through in order) at most 48 rows name the same one
- grad_out_b: bfloat16 [2, 1024, 3584], P('pipe', 'expert'), may hold values from -0.796875 to 0.796875
- router: bfloat16 [2, 16, 3584], P('pipe'), as said below
- w_up: bfloat16 [2, 16, 3584, 1024], P('pipe', 'expert'), as said below
- w_down: bfloat16 [2, 16, 1024, 3584], P('pipe', 'expert'), as said below
Outputs:
- layer_out_a: bfloat16 [2, 1024, 3584], P('pipe', 'expert')
- grad_in_b: bfloat16 [2, 1024, 3584], P('pipe', 'expert')
- router_grad: float32 [2, 16, 3584], P('pipe', 'expert')
The draws below stay inside these ranges and needn't reach their ends.
Inputs may be any that keep to these rules, and one draw needn't show every extreme that they name: `routes_a`: each token names 8 different experts. Among the 64 tokens of one device no expert is named by more than 48 tokens, and in every draw some expert is named by exactly 48 tokens of some device. `routes_b`: as for routes_a. router[1 - p] equals router[p] for every p. w_up[1 - p] equals w_up[p] for every p. w_down[1 - p] equals w_down[p] for every p.
All inputs are finite; a program needn't handle non-finite values.
Results may differ from the reference program's by a relative error of at most 0.014.
Values may be sent and summed in bfloat16 or wider, within the bound.
A program may use at most 128 MiB of HBM per device.

```python
import math
import jax
import jax.numpy as jnp
import numpy as np
from jax import lax

D = 3584
F = 1024
TOP = 8
TOK_DEV = 64
EXPERTS = 16
TOKENS = 1024
CAP = 48
N_PIPE = 2
N_EXPERT = 16


def mirrored_weight(key, inner_shape, fan_in):
    half_shape = (N_PIPE // 2,) + inner_shape
    scale = fan_in ** (-0.5)
    values = jnp.clip(jax.random.normal(key, half_shape, jnp.float32), -6.0, 6.0) * scale
    return jnp.concatenate([values, values[::-1]], axis=0)


def draw_router(key, part):
    return mirrored_weight(jax.random.fold_in(key, 11), (EXPERTS, D), D).astype(jnp.bfloat16)


def draw_w_up(key, part):
    return mirrored_weight(jax.random.fold_in(key, 23), (EXPERTS, D, F), D).astype(jnp.bfloat16)


def draw_w_down(key, part):
    return mirrored_weight(jax.random.fold_in(key, 37), (EXPERTS, F, D), F).astype(jnp.bfloat16)


def steps_of(rng, extent, shards, smallest, high):
    level = 1.0
    for axis_at, shards_of in shards:
        heights = jax.random.uniform(jax.random.fold_in(jax.random.fold_in(rng, 6), axis_at), (shards_of,), jnp.float32, smallest / len(shards), high / len(shards))
        level = level * jnp.repeat(jnp.exp(heights), extent[axis_at] // shards_of).reshape((-1,) + (1,) * (len(extent) - 1 - axis_at))
    return level


def shared_out(rng, own, number, rows, number_of, top, limit, lean):
    ranking = jax.random.permutation(rng, number_of)
    packed, usual = portions_of(number_of, rows * top, limit, lean, True), portions_of(number_of, rows * top, limit, lean, False)
    places = jnp.arange(number_of)

    def named(sizes, offset_by):
        used = int((sizes > 0).sum())
        fixed = max(1, used // 4)
        moved = fixed + (places - fixed + offset_by * (used - fixed)) % max(1, number_of - fixed)
        return jnp.zeros((number_of,), jnp.int32).at[ranking[jnp.where(places < fixed, places, moved)]].set(jnp.asarray(sizes, jnp.int32))

    sizes = jnp.where(number % 4 == 0, named(packed, number // 4), named(usual, number - number // 4 - 1))
    mixed = jax.random.permutation(jax.random.fold_in(own, 3), number_of)
    source_of, taker = mixed[0:number_of // 2 * 2:2], mixed[1:number_of // 2 * 2:2]
    room = jnp.minimum(sizes[source_of] - 1, limit - sizes[taker]) // 2
    room = jnp.where((source_of == ranking[0]) | (taker == ranking[0]) | (sizes[taker] == 0), 0, jnp.maximum(room, 0))
    moved = jax.random.randint(jax.random.fold_in(own, 4), (number_of // 2,), 0, 1 << 20) % (room + 1)
    sizes = sizes.at[source_of].add(-moved).at[taker].add(moved)
    items = jnp.searchsorted(jnp.cumsum(sizes), jnp.arange(rows * top), side="right").astype(jnp.int32)
    grid = items.reshape(top, rows).T
    grid = grid[jax.random.permutation(jax.random.fold_in(own, 1), rows)]
    offset_by = jax.random.randint(jax.random.fold_in(own, 2), (rows, 1), 0, top)
    return jnp.take_along_axis(grid, (jnp.arange(top)[None, :] + offset_by) % top, axis=1)


def portions_of(number_of, total, reach, slope, full):
    weights = [(1 << 20) // math.isqrt(standing ** slope) + 1 for standing in range(1, number_of + 1)]
    largest = reach if full else min(reach, max(-(-total // number_of), total * weights[0] // sum(weights)))
    least = 1 if total - largest >= number_of - 1 else 0
    given, spare = [largest] + [least] * (number_of - 1), total - largest - least * (number_of - 1)
    while spare > 0:
        movable = [i for i in range(1, number_of) if given[i] < largest] or [i for i in range(1, number_of) if given[i] < reach]
        pool, left = sum([weights[i] for i in movable]), spare
        for i in movable:
            more = min(reach - given[i], max(1, left * weights[i] // pool), spare)
            given[i] = given[i] + more
            spare = spare - more
    return np.array(given)


def centred(own_key, dims, scale, most, shards=(), kind=jnp.bfloat16):
    result = scale * jax.random.normal(own_key, dims, jnp.float32)
    if shards:
        result = result * steps_of(own_key, dims, shards, -0.22, 0.18)
    return jnp.clip(result, -most, most).astype(kind)


def setup_inputs(seed: int = 0) -> dict:
    key_list = jax.random.split(jax.random.key(seed), 9)
    hidden_a = centred(key_list[0], (N_PIPE, TOKENS, D), 1.0, 6.0, ((0, 2), (1, 16)))
    routes_a_keys = jax.random.split(jax.random.fold_in(key_list[1], 1), N_PIPE * TOKENS // TOK_DEV)
    routes_a_turns = jax.random.permutation(jax.random.fold_in(key_list[1], 3), N_PIPE * TOKENS // TOK_DEV)
    routes_a = jax.vmap(lambda own, number: shared_out(jax.random.fold_in(key_list[1], 2), own, number, TOK_DEV, EXPERTS, TOP, CAP, 2))(routes_a_keys, routes_a_turns).reshape((N_PIPE, TOKENS, TOP))
    hidden_b = centred(key_list[2], (N_PIPE, TOKENS, D), 1.0, 6.0, ((0, 2), (1, 16)))
    routes_b_keys = jax.random.split(jax.random.fold_in(key_list[3], 1), N_PIPE * TOKENS // TOK_DEV)
    routes_b_turns = jax.random.permutation(jax.random.fold_in(key_list[3], 3), N_PIPE * TOKENS // TOK_DEV)
    routes_b = jax.vmap(lambda own, number: shared_out(jax.random.fold_in(key_list[3], 2), own, number, TOK_DEV, EXPERTS, TOP, CAP, 2))(routes_b_keys, routes_b_turns).reshape((N_PIPE, TOKENS, TOP))
    grad_out_b = centred(key_list[4], (N_PIPE, TOKENS, D), 0.1, 0.796875, ((0, 2), (1, 16)))
    router = draw_router(jax.random.fold_in(key_list[8], 71), 0)
    w_up = draw_w_up(jax.random.fold_in(key_list[8], 71), 0)
    w_down = draw_w_down(jax.random.fold_in(key_list[8], 71), 0)
    return dict(hidden_a=hidden_a, routes_a=routes_a, hidden_b=hidden_b, routes_b=routes_b, grad_out_b=grad_out_b, router=router, w_up=w_up, w_down=w_down)


ROUTED_SCALE = 2.5
EPSILON = 1e-06

def silu_slope(pre):
    sig = jax.nn.sigmoid(pre)
    return sig * (1.0 + pre * (1.0 - sig))

def expert_table(routes_flat):
    slot_width = N_EXPERT * CAP
    onehot = (routes_flat[:, None] == jnp.arange(EXPERTS, dtype=jnp.int32)[None, :]).astype(jnp.int32)
    slot_rank = lax.optimization_barrier(jnp.sum((jnp.cumsum(onehot, axis=0) - 1) * onehot, axis=1))
    slot_index = routes_flat * slot_width + slot_rank
    pair_ids = jnp.arange(routes_flat.shape[0], dtype=jnp.int32)
    pair_table = jnp.zeros((EXPERTS * slot_width,), jnp.int32).at[slot_index].set(pair_ids)
    return (slot_index, pair_table.reshape(EXPERTS, slot_width))

def gate_weights(normed, routes, router_segment):
    logits = jnp.dot(normed, router_segment.T, preferred_element_type=jnp.float32)
    picked = jnp.take_along_axis(logits, routes, axis=1)
    affinity = jax.nn.sigmoid(picked)
    aff_total = lax.optimization_barrier(jnp.sum(affinity, axis=1, keepdims=True))
    return (affinity, aff_total, affinity / aff_total)

def forward_rows(normed, routes, up_segment, down_segment):
    slot_index, pair_table = expert_table(routes.reshape(-1))

    def per_expert(inputs):
        up_one, down_one, entries = inputs
        gathered = normed[entries // TOP]
        pre = jnp.dot(gathered, up_one, preferred_element_type=jnp.float32)
        active = jax.nn.silu(pre).astype(jnp.bfloat16)
        return jnp.dot(active, down_one, preferred_element_type=jnp.float32).astype(jnp.bfloat16)
    results = lax.map(per_expert, (up_segment, down_segment, pair_table))
    return results.reshape(-1, D)[slot_index].reshape(TOKENS, TOP, D)

def backward_rows(normed, grad_out, routes, up_segment, down_segment):
    slot_index, pair_table = expert_table(routes.reshape(-1))

    def per_expert(inputs):
        up_one, down_one, entries = inputs
        gathered = normed[entries // TOP]
        grad_rows = grad_out[entries // TOP]
        pre = jnp.dot(gathered, up_one, preferred_element_type=jnp.float32)
        active = jax.nn.silu(pre).astype(jnp.bfloat16)
        back = jnp.dot(grad_rows, down_one.T, preferred_element_type=jnp.float32)
        score = lax.optimization_barrier(jnp.sum(back * active.astype(jnp.float32), axis=-1)).astype(jnp.bfloat16)
        inner = (back * silu_slope(pre)).astype(jnp.bfloat16)
        lifted = jnp.dot(inner, up_one.T, preferred_element_type=jnp.float32).astype(jnp.bfloat16)
        return (lifted, score)
    lifted, score = lax.map(per_expert, (up_segment, down_segment, pair_table))
    lifted = lifted.reshape(-1, D)[slot_index].reshape(TOKENS, TOP, D)
    score = score.reshape(-1)[slot_index].reshape(TOKENS, TOP)
    return (lifted, score)

def reference(hidden_a, routes_a, hidden_b, routes_b, grad_out_b, router, w_up, w_down):
    outs_a = []
    grads_b = []
    terms = []
    for segment in range(N_PIPE):
        router_segment = router[segment]
        hidden32 = hidden_a[segment].astype(jnp.float32)
        rinv = lax.rsqrt(lax.optimization_barrier(jnp.mean(hidden32 * hidden32, axis=-1, keepdims=True)) + EPSILON)
        normed = (hidden32 * rinv).astype(jnp.bfloat16)
        affinity, aff_total, weight = gate_weights(normed, routes_a[segment], router_segment)
        expert_out = forward_rows(normed, routes_a[segment], w_up[segment], w_down[segment])
        mixed = hidden32 + ROUTED_SCALE * lax.optimization_barrier(jnp.sum(weight[:, :, None] * expert_out.astype(jnp.float32), axis=1))
        outs_a.append(mixed.astype(jnp.bfloat16))
        hidden32 = hidden_b[segment].astype(jnp.float32)
        rinv = lax.rsqrt(lax.optimization_barrier(jnp.mean(hidden32 * hidden32, axis=-1, keepdims=True)) + EPSILON)
        normed = (hidden32 * rinv).astype(jnp.bfloat16)
        affinity, aff_total, weight = gate_weights(normed, routes_b[segment], router_segment)
        lifted, score = backward_rows(normed, grad_out_b[segment], routes_b[segment], w_up[segment], w_down[segment])
        gate_grad = ROUTED_SCALE * score.astype(jnp.float32)
        logit_grad = affinity * (1.0 - affinity) * (gate_grad - lax.optimization_barrier(jnp.sum(gate_grad * weight, axis=1, keepdims=True))) / aff_total
        chosen = (routes_b[segment][:, :, None] == jnp.arange(EXPERTS, dtype=jnp.int32)[None, None, :]).astype(jnp.float32)
        dense = lax.optimization_barrier(jnp.sum(chosen * logit_grad[:, :, None], axis=1))
        normed_grad = ROUTED_SCALE * lax.optimization_barrier(jnp.sum(weight[:, :, None] * lifted.astype(jnp.float32), axis=1))
        normed_grad = normed_grad + jnp.dot(dense, router_segment.astype(jnp.float32), precision=lax.Precision.HIGHEST)
        mean_term = lax.optimization_barrier(jnp.mean(normed_grad * hidden32, axis=-1, keepdims=True))
        grad_in = grad_out_b[segment].astype(jnp.float32) + rinv * normed_grad - hidden32 * rinv ** 3 * mean_term
        grads_b.append(grad_in.astype(jnp.bfloat16))
        terms.append(jnp.dot(dense.T, normed.astype(jnp.float32), precision=lax.Precision.HIGHEST))
    router_grad = jnp.stack([terms[segment] + terms[N_PIPE - 1 - segment] for segment in range(N_PIPE)])
    return (jnp.stack(outs_a), jnp.stack(grads_b), router_grad)
```

```python
import jax
import jax.numpy as jnp
from jax import lax
from jax.sharding import PartitionSpec as P

ROUTED_SCALE = 2.5
EPSILON = 1e-06


def partner(block, axis, bit):
    count = lax.axis_size(axis)
    route = []
    for low in range(count):
        high = low | 1 << bit
        if high != low and high < count:
            route += [(low, high), (high, low)]
    return lax.ppermute(block, axis, route)


def gather(block):
    return lax.all_gather(block, "expert", axis=0, tiled=True)


def prepare(hidden, routes, router_segment):
    expert_count = router_segment.shape[0]
    hidden32 = hidden.astype(jnp.float32)
    rinv = lax.rsqrt(jnp.mean(hidden32 * hidden32, axis=-1, keepdims=True) + EPSILON)
    normed = (hidden32 * rinv).astype(jnp.bfloat16)
    logits = jnp.einsum("td,ed->te", normed, router_segment, preferred_element_type=jnp.float32)
    chosen = jnp.any(
        routes[:, :, None] == jnp.arange(expert_count, dtype=jnp.int32)[None, None, :], axis=1
    )
    affinity = jnp.where(chosen, jax.nn.sigmoid(logits), 0.0)
    return (hidden32, rinv, normed, affinity)


def on_device(hidden_a, routes_a, hidden_b, routes_b, grad_out_b, router, w_up, w_down):
    n_expert = lax.axis_size("expert")
    me = lax.axis_index("expert")
    tok_count = hidden_a.shape[1]
    router_segment = router[0]
    expert_count = router_segment.shape[0]
    local_count = w_up.shape[1]
    hidden32_a, rinv_a, normed_a, affinity_a = prepare(hidden_a[0], routes_a[0], router_segment)
    hidden32_b, rinv_b, normed_b, affinity_b = prepare(hidden_b[0], routes_b[0], router_segment)
    grad_out = grad_out_b[0]
    affinities = gather(jnp.concatenate([affinity_a, affinity_b], axis=1))
    rows_a = gather(normed_a)
    rows_b = gather(normed_b)
    rows_g = gather(grad_out)
    aff_a, aff_b = affinities[:, :expert_count], affinities[:, expert_count:]
    total_b = jnp.sum(aff_b, axis=1, keepdims=True)
    weight_a = aff_a / jnp.sum(aff_a, axis=1, keepdims=True)
    weight_b = aff_b / total_b

    def column(table, local):
        return lax.dynamic_slice_in_dim(table, me * local_count + local, 1, axis=1)

    sum_a = 0.0
    sum_b = 0.0
    scores = []
    for local in range(local_count):
        up, down = w_up[0, local], w_down[0, local]
        pre = jnp.dot(rows_a, up, preferred_element_type=jnp.float32)
        active = jax.nn.silu(pre).astype(jnp.bfloat16)
        out = jnp.dot(active, down, preferred_element_type=jnp.float32)
        sum_a = sum_a + out * column(weight_a, local)
    for local in range(local_count):
        up, down = w_up[0, local], w_down[0, local]
        pre = jnp.dot(rows_b, up, preferred_element_type=jnp.float32)
        back = jnp.einsum("td,fd->tf", rows_g, down, preferred_element_type=jnp.float32)
        sig = jax.nn.sigmoid(pre)
        scores.append(jnp.sum(back * (pre * sig), axis=-1))
        inner = (back * (sig * (1.0 + pre * (1.0 - sig)))).astype(jnp.bfloat16)
        lifted = jnp.einsum("tf,df->td", inner, up, preferred_element_type=jnp.float32)
        sum_b = sum_b + lifted * column(weight_b, local)
    mixed = lax.psum_scatter(
        sum_a.astype(jnp.bfloat16), "expert", scatter_dimension=0, tiled=True
    ).astype(jnp.float32)
    layer_out = (hidden32_a + ROUTED_SCALE * mixed).astype(jnp.bfloat16)

    score = gather(jnp.stack(scores)).T
    score = jnp.where(aff_b > 0.0, score, 0.0)
    gate_grad = ROUTED_SCALE * score
    logit_grad = (
        aff_b
        * (1.0 - aff_b)
        * (gate_grad - jnp.sum(gate_grad * weight_b, axis=1, keepdims=True))
        / total_b
    )
    own_columns = lax.dynamic_slice_in_dim(logit_grad, me * local_count, local_count, axis=1)
    own_term = jnp.dot(
        own_columns.T, rows_b.astype(jnp.float32), precision=lax.Precision.HIGHEST
    )
    mirrored = own_term
    for bit in range(lax.axis_size("pipe").bit_length() - 1):
        mirrored = partner(mirrored, "pipe", bit)
    router_grad = own_term + mirrored

    dense = lax.dynamic_slice_in_dim(logit_grad, me * tok_count, tok_count, axis=0)
    lifted_sum = lax.psum_scatter(
        sum_b.astype(jnp.bfloat16), "expert", scatter_dimension=0, tiled=True
    ).astype(jnp.float32)
    normed_grad = ROUTED_SCALE * lifted_sum + jnp.dot(
        dense, router_segment.astype(jnp.float32), precision=lax.Precision.HIGHEST
    )
    mean_term = jnp.mean(normed_grad * hidden32_b, axis=-1, keepdims=True)
    grad_in = (
        grad_out.astype(jnp.float32) + rinv_b * normed_grad - hidden32_b * rinv_b**3 * mean_term
    )
    return (layer_out[None], grad_in.astype(jnp.bfloat16)[None], router_grad[None])


def solution(mesh):
    placed = (
        P("pipe", "expert", None),
        P("pipe", "expert", None),
        P("pipe", "expert", None),
        P("pipe", "expert", None),
        P("pipe", "expert", None),
        P("pipe", None, None),
        P("pipe", "expert", None, None),
        P("pipe", "expert", None, None),
    )
    return jax.shard_map(
        on_device,
        mesh=mesh,
        in_specs=placed,
        out_specs=(P("pipe", "expert", None), P("pipe", "expert", None), P("pipe", "expert", None)),
        check_vma=False,
    )
```

```python
import functools

import jax
import jax.numpy as jnp
from jax import lax
from jax.experimental import pallas as pl
from jax.experimental.pallas import tpu as pltpu
from jax.sharding import PartitionSpec as P

ROUTED_SCALE = 2.5
EPSILON = 1e-06


def partner(block, axis, bit):
    count = lax.axis_size(axis)
    route = []
    for low in range(count):
        high = low | 1 << bit
        if high != low and high < count:
            route += [(low, high), (high, low)]
    return lax.ppermute(block, axis, route)


MESH = pl.DeviceIdType.MESH
DMA = pltpu.SemaphoreType.DMA
PLANE = 4


def remote(src, dst, send_sem, recv_sem, target):
    return pltpu.make_async_remote_copy(
        src_ref=src,
        dst_ref=dst,
        send_sem=send_sem,
        recv_sem=recv_sem,
        device_id={"expert": target},
        device_id_type=MESH,
    )


def place():
    me = lax.axis_index("expert")
    z, y, x = me // PLANE, (me // 2) % 2, me % 2
    return (me, z, y, x, me + 1 - 2 * x, me + 2 - 4 * y)


def greet(planes):
    me, z, y, x, x_near, y_near = place()
    barrier = pltpu.get_barrier_semaphore()
    pl.semaphore_signal(barrier, inc=1, device_id={"expert": x_near}, device_id_type=MESH)
    pl.semaphore_signal(barrier, inc=1, device_id={"expert": y_near}, device_id_type=MESH)

    @pl.when(z < planes - 1)
    def _():
        pl.semaphore_signal(barrier, inc=1, device_id={"expert": me + PLANE}, device_id_type=MESH)

    @pl.when(z > 0)
    def _():
        pl.semaphore_signal(barrier, inc=1, device_id={"expert": me - PLANE}, device_id_type=MESH)

    ends = jnp.where(z == 0, 1, 0) + jnp.where(z == planes - 1, 1, 0)
    pl.semaphore_wait(barrier, 4 - ends)


def gather_kernel(count, planes, *refs):
    ins, outs = refs[:count], refs[count : 2 * count]
    own_sem, up_s, down_s, z_r, x_s, x_r, y_s, y_r, d_s, d_r = refs[2 * count :]
    me, z, y, x, x_near, y_near = place()

    def up(k, p, src):
        return remote(src, outs[k].at[p * PLANE + y * 2 + x], up_s.at[k, p], z_r.at[k, p], me + PLANE)

    def down(k, p, src):
        return remote(src, outs[k].at[p * PLANE + y * 2 + x], down_s.at[k, p], z_r.at[k, p], me - PLANE)

    def to_x(k, p, src):
        return remote(src, outs[k].at[p * PLANE + y * 2 + x], x_s.at[k, p], x_r.at[k, p], x_near)

    def to_y(k, p, src):
        return remote(src, outs[k].at[p * PLANE + y * 2 + x], y_s.at[k, p], y_r.at[k, p], y_near)

    def half(k, p, way):
        if way == 0:
            ref = outs[k].at[p * PLANE + y * 2 + 1 - x, 0]
            return remote(ref, ref, d_s.at[k, p, 0], d_r.at[k, p, 0], y_near)
        ref = outs[k].at[p * PLANE + (1 - y) * 2 + x, 1]
        return remote(ref, ref, d_s.at[k, p, 1], d_r.at[k, p, 1], x_near)

    def each(d, act):
        if d == 0:
            act(z, 0)
            return

        @pl.when(z >= d)
        def _():
            act(z - d, 1)

        @pl.when(z + d < planes)
        def _():
            act(z + d, -1)

    def spread(k, p, way, wait):
        src = ins[k] if way == 0 else outs[k].at[p * PLANE + y * 2 + x]

        def do(copy):
            copy.wait_send() if wait else copy.start()

        if way != 0 and not wait:
            up(k, p, src).wait_recv()
        if way >= 0:

            @pl.when(z < planes - 1)
            def _():
                do(up(k, p, src))

        if way <= 0:

            @pl.when(z > 0)
            def _():
                do(down(k, p, src))

        do(to_x(k, p, src))
        do(to_y(k, p, src))

    def relay(k, p, way):
        to_x(k, p, ins[k]).wait_recv()
        half(k, p, 0).start()
        to_y(k, p, ins[k]).wait_recv()
        half(k, p, 1).start()

    def finish(k, p, way):
        for route in range(2):
            half(k, p, route).wait()
        spread(k, p, way, True)

    greet(planes)
    for k in range(count):
        pltpu.make_async_copy(ins[k], outs[k].at[me], own_sem.at[k]).start()
        each(0, lambda p, way: spread(k, p, way, False))
    for k in range(count):
        for d in range(1, planes):
            each(d, lambda p, way: spread(k, p, way, False))
            each(d - 1, lambda p, way: relay(k, p, way))
        each(planes - 1, lambda p, way: relay(k, p, way))
    for k in range(count):
        for d in range(planes):
            each(d, lambda p, way: finish(k, p, way))
        pltpu.make_async_copy(ins[k], outs[k].at[me], own_sem.at[k]).wait()


def gather_all(blocks, collective_id):
    n = lax.axis_size("expert")
    planes = n // PLANE
    count = len(blocks)
    halved = [b.reshape(2, b.shape[0] // 2, b.shape[1]) for b in blocks]
    outs = pl.pallas_call(
        functools.partial(gather_kernel, count, planes),
        out_shape=[jax.ShapeDtypeStruct((n,) + b.shape, b.dtype) for b in halved],
        in_specs=[pl.BlockSpec(memory_space=pltpu.VMEM)] * count,
        out_specs=[pl.BlockSpec(memory_space=pl.ANY)] * count,
        scratch_shapes=[DMA((count,))] + [DMA((count, planes))] * 7 + [DMA((count, planes, 2))] * 2,
        compiler_params=pltpu.CompilerParams(collective_id=collective_id, has_side_effects=True),
    )(*halved)
    return [o.reshape(n * b.shape[0], b.shape[1]) for o, b in zip(outs, blocks)]


def scatter_kernel(planes, part, out, a_r, c_r, b_x, b_y, total, z_r, *sems):
    ax_s, ax_r, ay_s, ay_r, cx_s, cx_r, cy_s, cy_r, z_s, up_r, down_r = sems
    me, z, y, x, x_near, y_near = place()
    rows, cols = part.shape[2:]
    step = 16

    def slot(p, yy, xx):
        return p * PLANE + yy * 2 + xx

    def add(dst, *srcs):
        def body(i, carry):
            r = pl.ds(pl.multiple_of(i * step, step), step)
            acc = srcs[0][r, :].astype(jnp.float32)
            for s in srcs[1:]:
                acc = acc + s[r, :].astype(jnp.float32)
            dst[r, :] = acc.astype(dst.dtype)
            return carry

        lax.fori_loop(0, rows // step, body, 0)

    def diagonal(p):
        src = slot(p, 1 - y, 1 - x)
        return (
            remote(part.at[src, 0], a_r.at[p, 0], ay_s.at[p], ay_r.at[p], y_near),
            remote(part.at[src, 1], a_r.at[p, 1], ax_s.at[p], ax_r.at[p], x_near),
        )

    def beside(p):
        return (
            remote(b_x.at[p, 0], c_r.at[p, 0, 0], cx_s.at[p, 0], cx_r.at[p, 0], x_near),
            remote(part.at[slot(p, y, 1 - x), 1], c_r.at[p, 0, 1], cx_s.at[p, 1], cx_r.at[p, 1], x_near),
            remote(b_y.at[p, 0], c_r.at[p, 1, 1], cy_s.at[p, 0], cy_r.at[p, 0], y_near),
            remote(part.at[slot(p, 1 - y, x), 0], c_r.at[p, 1, 0], cy_s.at[p, 1], cy_r.at[p, 1], y_near),
        )

    def rise(p):
        return remote(total.at[p], z_r.at[0, p], z_s.at[p], up_r.at[p], me + PLANE)

    def sink(p):
        return remote(total.at[p], z_r.at[1, p], z_s.at[p], down_r.at[p], me - PLANE)

    def each(d, act):
        if d == 0:
            act(z, 0)
            return

        @pl.when(z >= d)
        def _():
            act(z - d, -1)

        @pl.when(z + d < planes)
        def _():
            act(z + d, 1)

    def first(p, way):
        for copy in diagonal(p):
            copy.start()
        beside(p)[1].start()
        beside(p)[3].start()

    def second(p, way):
        to_y, to_x = diagonal(p)
        to_y.wait_recv()
        add(b_x.at[p, 0], part.at[slot(p, y, 1 - x), 0], a_r.at[p, 0])
        beside(p)[0].start()
        to_x.wait_recv()
        add(b_y.at[p, 0], part.at[slot(p, 1 - y, x), 1], a_r.at[p, 1])
        beside(p)[2].start()

    def third(p, way):
        for copy in beside(p):
            copy.wait_recv()
        for h in range(2):
            add(total.at[p, h], part.at[slot(p, y, x), h], c_r.at[p, 0, h], c_r.at[p, 1, h])

        def take(copy, level):
            copy.wait_recv()
            for h in range(2):
                add(total.at[p, h], total.at[p, h], z_r.at[level, p, h])

        if way >= 0:

            @pl.when(z > 0)
            def _():
                take(rise(p), 0)

        if way <= 0:

            @pl.when(z < planes - 1)
            def _():
                take(sink(p), 1)

        if way > 0:
            rise(p).start()
        if way < 0:
            sink(p).start()
        if way == 0:
            out[...] = total[p]

    def finish(p, way):
        for copy in diagonal(p) + beside(p):
            copy.wait_send()
        if way != 0:
            rise(p).wait_send()

    greet(planes)
    order = list(range(planes - 1, -1, -1))
    for d in order:
        each(d, first)
    for i, d in enumerate(order):
        each(d, second)
        if i > 0:
            each(order[i - 1], third)
    each(0, third)
    for d in order:
        each(d, finish)


def scatter_sum(part, collective_id):
    n = lax.axis_size("expert")
    planes = n // PLANE
    tokens, cols = part.shape
    rows = tokens // n // 2
    half = (rows, cols)
    kind = part.dtype
    out = pl.pallas_call(
        functools.partial(scatter_kernel, planes),
        out_shape=jax.ShapeDtypeStruct((2,) + half, kind),
        in_specs=[pl.BlockSpec(memory_space=pltpu.VMEM)],
        out_specs=pl.BlockSpec(memory_space=pltpu.VMEM),
        scratch_shapes=[
            pltpu.VMEM((planes, 2) + half, kind),
            pltpu.VMEM((planes, 2, 2) + half, kind),
            pltpu.VMEM((planes, 1) + half, kind),
            pltpu.VMEM((planes, 1) + half, kind),
            pltpu.VMEM((planes, 2) + half, kind),
            pltpu.VMEM((2, planes, 2) + half, kind),
        ]
        + [DMA((planes,))] * 4
        + [DMA((planes, 2))] * 4
        + [DMA((planes,))] * 3,
        compiler_params=pltpu.CompilerParams(
            collective_id=collective_id, has_side_effects=True, vmem_limit_bytes=60 << 20
        ),
    )(part.reshape((n, 2) + half))
    return out.reshape(2 * rows, cols)


def prepare(hidden, routes, router_segment):
    expert_count = router_segment.shape[0]
    hidden32 = hidden.astype(jnp.float32)
    rinv = lax.rsqrt(jnp.mean(hidden32 * hidden32, axis=-1, keepdims=True) + EPSILON)
    normed = (hidden32 * rinv).astype(jnp.bfloat16)
    logits = jnp.einsum("td,ed->te", normed, router_segment, preferred_element_type=jnp.float32)
    chosen = jnp.any(
        routes[:, :, None] == jnp.arange(expert_count, dtype=jnp.int32)[None, None, :], axis=1
    )
    affinity = jnp.where(chosen, jax.nn.sigmoid(logits), 0.0)
    return (hidden32, rinv, normed, affinity)


def on_device(hidden_a, routes_a, hidden_b, routes_b, grad_out_b, router, w_up, w_down):
    n_expert = lax.axis_size("expert")
    me = lax.axis_index("expert")
    tok_count = hidden_a.shape[1]
    router_segment = router[0]
    expert_count = router_segment.shape[0]
    local_count = w_up.shape[1]
    hidden32_a, rinv_a, normed_a, affinity_a = prepare(hidden_a[0], routes_a[0], router_segment)
    hidden32_b, rinv_b, normed_b, affinity_b = prepare(hidden_b[0], routes_b[0], router_segment)
    grad_out = grad_out_b[0]
    affinity_ab = jnp.concatenate([affinity_a, affinity_b], axis=1)
    lanes = -(-2 * expert_count // 128) * 128
    affinity_ab = jnp.pad(affinity_ab, ((0, 0), (0, lanes - 2 * expert_count)))
    rows_a, rows_b, rows_g, affinities = gather_all([normed_a, normed_b, grad_out, affinity_ab], 1)
    aff_a, aff_b = affinities[:, :expert_count], affinities[:, expert_count : 2 * expert_count]
    total_b = jnp.sum(aff_b, axis=1, keepdims=True)
    weight_a = aff_a / jnp.sum(aff_a, axis=1, keepdims=True)
    weight_b = aff_b / total_b

    def column(table, local):
        return lax.dynamic_slice_in_dim(table, me * local_count + local, 1, axis=1)

    sum_a = 0.0
    sum_b = 0.0
    scores = []
    for local in range(local_count):
        up, down = w_up[0, local], w_down[0, local]
        pre = jnp.dot(rows_a, up, preferred_element_type=jnp.float32)
        active = jax.nn.silu(pre).astype(jnp.bfloat16)
        out = jnp.dot(active, down, preferred_element_type=jnp.float32)
        sum_a = sum_a + out * column(weight_a, local)
    for local in range(local_count):
        up, down = w_up[0, local], w_down[0, local]
        pre = jnp.dot(rows_b, up, preferred_element_type=jnp.float32)
        back = jnp.einsum("td,fd->tf", rows_g, down, preferred_element_type=jnp.float32)
        sig = jax.nn.sigmoid(pre)
        scores.append(jnp.sum(back * (pre * sig), axis=-1))
        inner = (back * (sig * (1.0 + pre * (1.0 - sig)))).astype(jnp.bfloat16)
        lifted = jnp.einsum("tf,df->td", inner, up, preferred_element_type=jnp.float32)
        sum_b = sum_b + lifted * column(weight_b, local)
    mixed = scatter_sum(sum_a.astype(jnp.bfloat16), 2).astype(jnp.float32)
    layer_out = (hidden32_a + ROUTED_SCALE * mixed).astype(jnp.bfloat16)

    flat = jnp.stack(scores).reshape(-1)
    padded = jnp.pad(flat, (0, -flat.shape[0] % 2048)).reshape(-1, 128)
    score = gather_all([padded], 4)[0].reshape(n_expert, -1)[:, : flat.shape[0]]
    score = score.reshape(expert_count, -1).T
    score = jnp.where(aff_b > 0.0, score, 0.0)
    gate_grad = ROUTED_SCALE * score
    logit_grad = (
        aff_b
        * (1.0 - aff_b)
        * (gate_grad - jnp.sum(gate_grad * weight_b, axis=1, keepdims=True))
        / total_b
    )
    own_columns = lax.dynamic_slice_in_dim(logit_grad, me * local_count, local_count, axis=1)
    own_term = jnp.dot(
        own_columns.T, rows_b.astype(jnp.float32), precision=lax.Precision.HIGHEST
    )
    mirrored = own_term
    for bit in range(lax.axis_size("pipe").bit_length() - 1):
        mirrored = partner(mirrored, "pipe", bit)
    router_grad = own_term + mirrored

    dense = lax.dynamic_slice_in_dim(logit_grad, me * tok_count, tok_count, axis=0)
    lifted_sum = scatter_sum(sum_b.astype(jnp.bfloat16), 3).astype(jnp.float32)
    normed_grad = ROUTED_SCALE * lifted_sum + jnp.dot(
        dense, router_segment.astype(jnp.float32), precision=lax.Precision.HIGHEST
    )
    mean_term = jnp.mean(normed_grad * hidden32_b, axis=-1, keepdims=True)
    grad_in = (
        grad_out.astype(jnp.float32) + rinv_b * normed_grad - hidden32_b * rinv_b**3 * mean_term
    )
    return (layer_out[None], grad_in.astype(jnp.bfloat16)[None], router_grad[None])


def solution(mesh):
    placed = (
        P("pipe", "expert", None),
        P("pipe", "expert", None),
        P("pipe", "expert", None),
        P("pipe", "expert", None),
        P("pipe", "expert", None),
        P("pipe", None, None),
        P("pipe", "expert", None, None),
        P("pipe", "expert", None, None),
    )
    return jax.shard_map(
        on_device,
        mesh=mesh,
        in_specs=placed,
        out_specs=(P("pipe", "expert", None), P("pipe", "expert", None), P("pipe", "expert", None)),
        check_vma=False,
    )
```

```python
import functools

import jax
import jax.numpy as jnp
from jax import lax
from jax.experimental import pallas as pl
from jax.experimental.pallas import tpu as pltpu
from jax.sharding import PartitionSpec as P

ROUTED_SCALE = 2.5
EPSILON = 1e-06


def partner(block, axis, bit):
    count = lax.axis_size(axis)
    route = []
    for low in range(count):
        high = low | 1 << bit
        if high != low and high < count:
            route += [(low, high), (high, low)]
    return lax.ppermute(block, axis, route)


MESH = pl.DeviceIdType.MESH
DMA = pltpu.SemaphoreType.DMA
PLANE = 4


def remote(src, dst, send_sem, recv_sem, target):
    return pltpu.make_async_remote_copy(
        src_ref=src,
        dst_ref=dst,
        send_sem=send_sem,
        recv_sem=recv_sem,
        device_id={"expert": target},
        device_id_type=MESH,
    )


def place():
    me = lax.axis_index("expert")
    z, y, x = me // PLANE, (me // 2) % 2, me % 2
    return (me, z, y, x, me + 1 - 2 * x, me + 2 - 4 * y)


def greet(planes):
    me, z, y, x, x_near, y_near = place()
    barrier = pltpu.get_barrier_semaphore()
    pl.semaphore_signal(barrier, inc=1, device_id={"expert": x_near}, device_id_type=MESH)
    pl.semaphore_signal(barrier, inc=1, device_id={"expert": y_near}, device_id_type=MESH)

    @pl.when(z < planes - 1)
    def _():
        pl.semaphore_signal(barrier, inc=1, device_id={"expert": me + PLANE}, device_id_type=MESH)

    @pl.when(z > 0)
    def _():
        pl.semaphore_signal(barrier, inc=1, device_id={"expert": me - PLANE}, device_id_type=MESH)

    ends = jnp.where(z == 0, 1, 0) + jnp.where(z == planes - 1, 1, 0)
    pl.semaphore_wait(barrier, 4 - ends)


def gather_kernel(count, planes, *refs):
    ins, outs = refs[:count], refs[count : 2 * count]
    own_sem, up_s, down_s, z_r, x_s, x_r, y_s, y_r, d_s, d_r = refs[2 * count :]
    me, z, y, x, x_near, y_near = place()

    def up(k, p, src):
        return remote(src, outs[k].at[p * PLANE + y * 2 + x], up_s.at[k, p], z_r.at[k, p], me + PLANE)

    def down(k, p, src):
        return remote(src, outs[k].at[p * PLANE + y * 2 + x], down_s.at[k, p], z_r.at[k, p], me - PLANE)

    def to_x(k, p, src):
        return remote(src, outs[k].at[p * PLANE + y * 2 + x], x_s.at[k, p], x_r.at[k, p], x_near)

    def to_y(k, p, src):
        return remote(src, outs[k].at[p * PLANE + y * 2 + x], y_s.at[k, p], y_r.at[k, p], y_near)

    def half(k, p, way):
        if way == 0:
            ref = outs[k].at[p * PLANE + y * 2 + 1 - x, 0]
            return remote(ref, ref, d_s.at[k, p, 0], d_r.at[k, p, 0], y_near)
        ref = outs[k].at[p * PLANE + (1 - y) * 2 + x, 1]
        return remote(ref, ref, d_s.at[k, p, 1], d_r.at[k, p, 1], x_near)

    def each(d, act):
        if d == 0:
            act(z, 0)
            return

        @pl.when(z >= d)
        def _():
            act(z - d, 1)

        @pl.when(z + d < planes)
        def _():
            act(z + d, -1)

    def spread(k, p, way, wait):
        src = ins[k] if way == 0 else outs[k].at[p * PLANE + y * 2 + x]

        def do(copy):
            copy.wait_send() if wait else copy.start()

        if way != 0 and not wait:
            up(k, p, src).wait_recv()
        if way >= 0:

            @pl.when(z < planes - 1)
            def _():
                do(up(k, p, src))

        if way <= 0:

            @pl.when(z > 0)
            def _():
                do(down(k, p, src))

        do(to_x(k, p, src))
        do(to_y(k, p, src))

    def relay(k, p, way):
        to_x(k, p, ins[k]).wait_recv()
        half(k, p, 0).start()
        to_y(k, p, ins[k]).wait_recv()
        half(k, p, 1).start()

    def finish(k, p, way):
        for route in range(2):
            half(k, p, route).wait()
        spread(k, p, way, True)

    greet(planes)
    for k in range(count):
        pltpu.make_async_copy(ins[k], outs[k].at[me], own_sem.at[k]).start()
        each(0, lambda p, way: spread(k, p, way, False))
    for k in range(count):
        for d in range(1, planes):
            each(d, lambda p, way: spread(k, p, way, False))
            each(d - 1, lambda p, way: relay(k, p, way))
        each(planes - 1, lambda p, way: relay(k, p, way))
    for k in range(count):
        for d in range(planes):
            each(d, lambda p, way: finish(k, p, way))
        pltpu.make_async_copy(ins[k], outs[k].at[me], own_sem.at[k]).wait()


def gather_all(blocks, collective_id):
    n = lax.axis_size("expert")
    planes = n // PLANE
    count = len(blocks)
    halved = [b.reshape(2, b.shape[0] // 2, b.shape[1]) for b in blocks]
    outs = pl.pallas_call(
        functools.partial(gather_kernel, count, planes),
        out_shape=[jax.ShapeDtypeStruct((n,) + b.shape, b.dtype) for b in halved],
        in_specs=[pl.BlockSpec(memory_space=pltpu.VMEM)] * count,
        out_specs=[pl.BlockSpec(memory_space=pl.ANY)] * count,
        scratch_shapes=[DMA((count,))] + [DMA((count, planes))] * 7 + [DMA((count, planes, 2))] * 2,
        compiler_params=pltpu.CompilerParams(collective_id=collective_id, has_side_effects=True),
    )(*halved)
    return [o.reshape(n * b.shape[0], b.shape[1]) for o, b in zip(outs, blocks)]


def scatter_stages(planes, part, out, a_r, c_r, b_x, b_y, total, z_r, *sems):
    ax_s, ax_r, ay_s, ay_r, cx_s, cx_r, cy_s, cy_r, z_s, up_r, down_r = sems
    me, z, y, x, x_near, y_near = place()
    rows, cols = part.shape[2:]
    step = 16

    def slot(p, yy, xx):
        return p * PLANE + yy * 2 + xx

    def add(dst, *srcs):
        def body(i, carry):
            r = pl.ds(pl.multiple_of(i * step, step), step)
            acc = srcs[0][r, :].astype(jnp.float32)
            for s in srcs[1:]:
                acc = acc + s[r, :].astype(jnp.float32)
            dst[r, :] = acc.astype(dst.dtype)
            return carry

        lax.fori_loop(0, rows // step, body, 0)

    def diagonal(p):
        src = slot(p, 1 - y, 1 - x)
        return (
            remote(part.at[src, 0], a_r.at[p, 0], ay_s.at[p], ay_r.at[p], y_near),
            remote(part.at[src, 1], a_r.at[p, 1], ax_s.at[p], ax_r.at[p], x_near),
        )

    def beside(p):
        return (
            remote(b_x.at[p, 0], c_r.at[p, 0, 0], cx_s.at[p, 0], cx_r.at[p, 0], x_near),
            remote(part.at[slot(p, y, 1 - x), 1], c_r.at[p, 0, 1], cx_s.at[p, 1], cx_r.at[p, 1], x_near),
            remote(b_y.at[p, 0], c_r.at[p, 1, 1], cy_s.at[p, 0], cy_r.at[p, 0], y_near),
            remote(part.at[slot(p, 1 - y, x), 0], c_r.at[p, 1, 0], cy_s.at[p, 1], cy_r.at[p, 1], y_near),
        )

    def rise(p):
        return remote(total.at[p], z_r.at[0, p], z_s.at[p], up_r.at[p], me + PLANE)

    def sink(p):
        return remote(total.at[p], z_r.at[1, p], z_s.at[p], down_r.at[p], me - PLANE)

    def first(p, way):
        for copy in diagonal(p):
            copy.start()
        beside(p)[1].start()
        beside(p)[3].start()

    def second(p, way):
        to_y, to_x = diagonal(p)
        to_y.wait_recv()
        add(b_x.at[p, 0], part.at[slot(p, y, 1 - x), 0], a_r.at[p, 0])
        beside(p)[0].start()
        to_x.wait_recv()
        add(b_y.at[p, 0], part.at[slot(p, 1 - y, x), 1], a_r.at[p, 1])
        beside(p)[2].start()

    def third(p, way):
        for copy in beside(p):
            copy.wait_recv()
        for h in range(2):
            add(total.at[p, h], part.at[slot(p, y, x), h], c_r.at[p, 0, h], c_r.at[p, 1, h])

        def take(copy, level):
            copy.wait_recv()
            for h in range(2):
                add(total.at[p, h], total.at[p, h], z_r.at[level, p, h])

        if way >= 0:

            @pl.when(z > 0)
            def _():
                take(rise(p), 0)

        if way <= 0:

            @pl.when(z < planes - 1)
            def _():
                take(sink(p), 1)

        if way > 0:
            rise(p).start()
        if way < 0:
            sink(p).start()
        if way == 0:
            out[...] = total[p]

    def finish(p, way):
        for copy in diagonal(p) + beside(p):
            copy.wait_send()
        if way != 0:
            rise(p).wait_send()

    return (first, second, third, finish)


def scatter_kernel(planes, count, *refs):
    parts, outs, rest = refs[:count], refs[count : 2 * count], refs[2 * count :]
    per = len(rest) // count
    z = place()[1]
    stages = [
        scatter_stages(planes, parts[k], outs[k], *rest[k * per : (k + 1) * per])
        for k in range(count)
    ]

    def each(d, act):
        if d == 0:
            act(z, 0)
            return

        @pl.when(z >= d)
        def _():
            act(z - d, -1)

        @pl.when(z + d < planes)
        def _():
            act(z + d, 1)

    greet(planes)
    order = list(range(planes - 1, -1, -1))
    for k in range(count):
        for d in order:
            each(d, stages[k][0])
    for i, d in enumerate(order):
        for k in range(count):
            each(d, stages[k][1])
        if i > 0:
            for k in range(count):
                each(order[i - 1], stages[k][2])
    for k in range(count):
        each(0, stages[k][2])
    for k in range(count):
        for d in order:
            each(d, stages[k][3])


def scatter_sums(parts, collective_id):
    n = lax.axis_size("expert")
    planes = n // PLANE
    tokens, cols = parts[0].shape
    rows = tokens // n // 2
    half = (rows, cols)
    kind = parts[0].dtype
    count = len(parts)
    if count > 1 and count * 3 * parts[0].size * kind.itemsize > 56 << 20:
        return [scatter_sums([part], collective_id + k)[0] for k, part in enumerate(parts)]
    outs = pl.pallas_call(
        functools.partial(scatter_kernel, planes, count),
        out_shape=[jax.ShapeDtypeStruct((2,) + half, kind)] * count,
        in_specs=[pl.BlockSpec(memory_space=pltpu.VMEM)] * count,
        out_specs=[pl.BlockSpec(memory_space=pltpu.VMEM)] * count,
        scratch_shapes=(
            [
                pltpu.VMEM((planes, 2) + half, kind),
                pltpu.VMEM((planes, 2, 2) + half, kind),
                pltpu.VMEM((planes, 1) + half, kind),
                pltpu.VMEM((planes, 1) + half, kind),
                pltpu.VMEM((planes, 2) + half, kind),
                pltpu.VMEM((2, planes, 2) + half, kind),
            ]
            + [DMA((planes,))] * 4
            + [DMA((planes, 2))] * 4
            + [DMA((planes,))] * 3
        )
        * count,
        compiler_params=pltpu.CompilerParams(
            collective_id=collective_id, has_side_effects=True, vmem_limit_bytes=60 << 20
        ),
    )(*[part.reshape((n, 2) + half) for part in parts])
    return [out.reshape(2 * rows, cols) for out in outs]


def prepare(hidden, routes, router_segment):
    expert_count = router_segment.shape[0]
    hidden32 = hidden.astype(jnp.float32)
    rinv = lax.rsqrt(jnp.mean(hidden32 * hidden32, axis=-1, keepdims=True) + EPSILON)
    normed = (hidden32 * rinv).astype(jnp.bfloat16)
    logits = jnp.einsum("td,ed->te", normed, router_segment, preferred_element_type=jnp.float32)
    chosen = jnp.any(
        routes[:, :, None] == jnp.arange(expert_count, dtype=jnp.int32)[None, None, :], axis=1
    )
    affinity = jnp.where(chosen, jax.nn.sigmoid(logits), 0.0)
    return (hidden32, rinv, normed, affinity)


def on_device(hidden_a, routes_a, hidden_b, routes_b, grad_out_b, router, w_up, w_down):
    n_expert = lax.axis_size("expert")
    me = lax.axis_index("expert")
    tok_count = hidden_a.shape[1]
    router_segment = router[0]
    expert_count = router_segment.shape[0]
    local_count = w_up.shape[1]
    hidden32_a, rinv_a, normed_a, affinity_a = prepare(hidden_a[0], routes_a[0], router_segment)
    hidden32_b, rinv_b, normed_b, affinity_b = prepare(hidden_b[0], routes_b[0], router_segment)
    grad_out = grad_out_b[0]
    affinity_ab = jnp.concatenate([affinity_a, affinity_b], axis=1)
    lanes = -(-2 * expert_count // 128) * 128
    affinity_ab = jnp.pad(affinity_ab, ((0, 0), (0, lanes - 2 * expert_count)))
    rows_a, rows_b, rows_g, affinities = gather_all([normed_a, normed_b, grad_out, affinity_ab], 1)
    aff_a, aff_b = affinities[:, :expert_count], affinities[:, expert_count : 2 * expert_count]
    total_b = jnp.sum(aff_b, axis=1, keepdims=True)
    weight_a = aff_a / jnp.sum(aff_a, axis=1, keepdims=True)
    weight_b = aff_b / total_b

    def column(table, local):
        return lax.dynamic_slice_in_dim(table, me * local_count + local, 1, axis=1)

    sum_a = 0.0
    sum_b = 0.0
    scores = []
    for local in range(local_count):
        up, down = w_up[0, local], w_down[0, local]
        pre = jnp.dot(rows_a, up, preferred_element_type=jnp.float32)
        active = jax.nn.silu(pre).astype(jnp.bfloat16)
        out = jnp.dot(active, down, preferred_element_type=jnp.float32)
        sum_a = sum_a + out * column(weight_a, local)
    for local in range(local_count):
        up, down = w_up[0, local], w_down[0, local]
        pre = jnp.dot(rows_b, up, preferred_element_type=jnp.float32)
        back = jnp.einsum("td,fd->tf", rows_g, down, preferred_element_type=jnp.float32)
        sig = jax.nn.sigmoid(pre)
        scores.append(jnp.sum(back * (pre * sig), axis=-1))
        inner = (back * (sig * (1.0 + pre * (1.0 - sig)))).astype(jnp.bfloat16)
        lifted = jnp.einsum("tf,df->td", inner, up, preferred_element_type=jnp.float32)
        sum_b = sum_b + lifted * column(weight_b, local)
    sum_ab = scatter_sums([sum_a.astype(jnp.bfloat16), sum_b.astype(jnp.bfloat16)], 2)
    mixed = sum_ab[0].astype(jnp.float32)
    layer_out = (hidden32_a + ROUTED_SCALE * mixed).astype(jnp.bfloat16)

    flat = jnp.stack(scores).reshape(-1)
    padded = jnp.pad(flat, (0, -flat.shape[0] % 2048)).reshape(-1, 128)
    score = gather_all([padded], 4)[0].reshape(n_expert, -1)[:, : flat.shape[0]]
    score = score.reshape(expert_count, -1).T
    score = jnp.where(aff_b > 0.0, score, 0.0)
    gate_grad = ROUTED_SCALE * score
    logit_grad = (
        aff_b
        * (1.0 - aff_b)
        * (gate_grad - jnp.sum(gate_grad * weight_b, axis=1, keepdims=True))
        / total_b
    )
    own_columns = lax.dynamic_slice_in_dim(logit_grad, me * local_count, local_count, axis=1)
    own_term = jnp.dot(
        own_columns.T, rows_b.astype(jnp.float32), precision=lax.Precision.HIGHEST
    )
    mirrored = own_term
    for bit in range(lax.axis_size("pipe").bit_length() - 1):
        mirrored = partner(mirrored, "pipe", bit)
    router_grad = own_term + mirrored

    dense = lax.dynamic_slice_in_dim(logit_grad, me * tok_count, tok_count, axis=0)
    lifted_sum = sum_ab[1].astype(jnp.float32)
    normed_grad = ROUTED_SCALE * lifted_sum + jnp.dot(
        dense, router_segment.astype(jnp.float32), precision=lax.Precision.HIGHEST
    )
    mean_term = jnp.mean(normed_grad * hidden32_b, axis=-1, keepdims=True)
    grad_in = (
        grad_out.astype(jnp.float32) + rinv_b * normed_grad - hidden32_b * rinv_b**3 * mean_term
    )
    return (layer_out[None], grad_in.astype(jnp.bfloat16)[None], router_grad[None])


def solution(mesh):
    placed = (
        P("pipe", "expert", None),
        P("pipe", "expert", None),
        P("pipe", "expert", None),
        P("pipe", "expert", None),
        P("pipe", "expert", None),
        P("pipe", None, None),
        P("pipe", "expert", None, None),
        P("pipe", "expert", None, None),
    )
    return jax.shard_map(
        on_device,
        mesh=mesh,
        in_specs=placed,
        out_specs=(P("pipe", "expert", None), P("pipe", "expert", None), P("pipe", "expert", None)),
        check_vma=False,
    )
```
